128 devices in a mesh: row: 8 (over y, z_hi), col: 16 (over x, z_lo, core).
Axes of the slice: x: 4, y: 4, z: 4 (z_hi: 2, z_lo: 2; z = z_hi * 2 + z_lo), core: 2. Of those that a mesh axis runs over, the one named last changes fastest.
Arguments:
- adjacency: bfloat16 [32768, 32768], P('row', 'col'), as said below
- tile_mask: int32 [256, 256], P('row', 'col'), may hold values from 0 to 1, as said below
- out_grad: bfloat16 [32768, 256], P(('row', 'col')), may hold values from -6 to 6
- pre_two: bfloat16 [32768, 256], P(('row', 'col')), may hold values from -6 to 6
- hidden: bfloat16 [32768, 256], P(('col', 'row')), may hold values from -24 to 24
- pre_one: bfloat16 [32768, 256], P(('col', 'row')), may hold values from -6 to 6
- features: bfloat16 [32768, 256], P(('row', 'col')), may hold values from -6 to 6
- w_two: bfloat16 [256, 256], replicated, may hold values from -0.375 to 0.375
- w_one: bfloat16 [256, 256], replicated, may hold values from -0.375 to 0.375
Outputs:
- node_grad: bfloat16 [32768, 256], P(('row', 'col'))
- weight_grad_one: float32 [256, 256], replicated
- weight_grad_two: float32 [256, 256], replicated
The draws below stay inside these ranges and needn't reach their ends.
Inputs may be any that keep to these rules, and one draw needn't show every extreme that they name: adjacency is symmetric and nonnegative. tile_mask is symmetric and every diagonal tile is 1.
All inputs are finite; a program needn't handle non-finite values.
Results may differ from the reference program's by a relative error of at most 0.02.
Values may be sent and summed in bfloat16 or wider, within the bound.
A program may use at most 128 MiB of HBM per device.

```python
import math
import jax
import jax.numpy as jnp
from jax import lax

F = 256
TILE = 128
NODE_DEV = 256
NODES = 32768
N_ROW = 8
N_COL = 16


def draw_adjacency(key, part):
    levels = jax.random.randint(key, (NODES, NODES), 0, 20480)
    kept_scale = 2.0 / math.sqrt(0.05 * NODES)
    values = (0.5 + levels.astype(jnp.float32) * (1.0 / 1024.0)) * kept_scale
    upper = jnp.where(levels < 1024, values, jnp.zeros_like(values))
    row_ids = lax.broadcasted_iota(jnp.int32, (NODES, 1), 0)
    col_ids = lax.broadcasted_iota(jnp.int32, (1, NODES), 1)
    symmetric = jnp.where(row_ids <= col_ids, upper, upper.T)
    return symmetric.astype(jnp.bfloat16)


def draw_tile_mask(key, part):
    tile_count = NODES // TILE
    group_count = 8
    levels = jax.random.randint(jax.random.fold_in(key, 1), (group_count,), 1, 9)
    group_ids = lax.broadcasted_iota(jnp.int32, (tile_count,), 0) * group_count // tile_count
    group_onehot = (group_ids[:, None] == jnp.arange(group_count, dtype=jnp.int32)[None, :]).astype(jnp.int32)
    tile_level = jnp.sum(group_onehot * levels[None, :], axis=1)
    odds = tile_level[:, None] * tile_level[None, :]
    tosses = jax.random.randint(jax.random.fold_in(key, 2), (tile_count, tile_count), 0, 64)
    hits = (tosses < odds).astype(jnp.int32)
    row_ids = lax.broadcasted_iota(jnp.int32, (tile_count, 1), 0)
    col_ids = lax.broadcasted_iota(jnp.int32, (1, tile_count), 1)
    symmetric = jnp.where(row_ids <= col_ids, hits, hits.T)
    return jnp.where(row_ids == col_ids, jnp.ones_like(symmetric), symmetric).astype(jnp.int32)


def strengthened(drawn, key, source, target, blocks, factor):
    owner, partner = [(jnp.arange(drawn.shape[position]) // (drawn.shape[position] // blocks)).reshape([-1 if axis == position else 1 for axis in range(drawn.ndim)]) for position in (source, target)]
    chosen = jax.random.permutation(key, blocks)[partner]
    strong = (owner == chosen) | (owner == (partner + blocks // 2) % blocks)
    return jnp.where(strong, factor * drawn, drawn)


def steps_of(key, dims, split, low, high):
    gain = 1.0
    for dim, blocks in split:
        heights = jax.random.uniform(jax.random.fold_in(jax.random.fold_in(key, 6), dim), (blocks,), jnp.float32, low / len(split), high / len(split))
        gain = gain * jnp.repeat(jnp.exp(heights), dims[dim] // blocks).reshape((-1,) + (1,) * (len(dims) - 1 - dim))
    return gain


def scatter_about(rng, extent, scale, most, cuts=(), held_as=jnp.bfloat16):
    result = jax.random.normal(rng, extent, jnp.float32) * scale
    if len(cuts) > 0:
        result = steps_of(rng, extent, cuts, -0.22, 0.18) * result
    return jnp.clip(result, min=-most, max=most).astype(held_as)


def heavy_noise(key, extent, deviation, most, cuts, heavy, held_as=jnp.bfloat16):
    array = deviation * jax.random.normal(key, extent, jnp.float32)
    if cuts:
        array = array * steps_of(key, extent, cuts, -0.22, 0.18)
    return jnp.clip(strengthened(array, jax.random.fold_in(key, 3), *heavy), -most, most).astype(held_as)


def setup_inputs(seed: int = 0) -> dict:
    seeds = jax.random.split(jax.random.key(seed), 10)
    return {
        "adjacency": draw_adjacency(jax.random.fold_in(seeds[9], 71), 0),
        "tile_mask": draw_tile_mask(jax.random.fold_in(seeds[9], 71), 0),
        "out_grad": scatter_about(seeds[2], (NODES, F), 1.0, 6.0, ((0, 128),)),
        "pre_two": scatter_about(seeds[3], (NODES, F), 1.0, 6.0, ((0, 128),)),
        "hidden": heavy_noise(seeds[4], (NODES, F), 1.0, 24.0, ((0, 128),), (0, 1, 128, 5.5)),
        "pre_one": scatter_about(seeds[5], (NODES, F), 1.0, 6.0, ((0, 128),)),
        "features": scatter_about(seeds[6], (NODES, F), 1.0, 6.0, ((0, 128),)),
        "w_two": scatter_about(seeds[7], (F, F), F ** -0.5, 0.375),
        "w_one": scatter_about(seeds[8], (F, F), F ** -0.5, 0.375),
    }


def propagate(adjacency, tile_mask, gradient, groups):
    node_count = adjacency.shape[0]
    tile_size = node_count // tile_mask.shape[0]
    block_rows = math.gcd(node_count, 2048)
    width = gradient.shape[1]
    group_nodes = node_count // groups
    dense_grad = gradient.astype(jnp.float32).reshape(groups, group_nodes, width)

    def block_product(block_index):
        graph_rows = lax.dynamic_slice_in_dim(adjacency, block_index * block_rows, block_rows, 0)
        mask_rows = lax.dynamic_slice_in_dim(tile_mask, block_index * (block_rows // tile_size), block_rows // tile_size, 0)
        mask_full = jnp.repeat(jnp.repeat(mask_rows.astype(jnp.float32), tile_size, 0), tile_size, 1)
        weighted = (graph_rows.astype(jnp.float32) * mask_full).reshape(block_rows, groups, group_nodes)
        partial_terms = jnp.einsum("bgk,gkf->gbf", weighted, dense_grad, precision=lax.Precision.HIGHEST)
        rounded = lax.optimization_barrier(partial_terms.astype(jnp.bfloat16))
        return jnp.sum(rounded.astype(jnp.float32), axis=0)

    indices = jnp.arange(node_count // block_rows).astype(jnp.int32)
    return lax.map(block_product, indices).reshape(node_count, width)


def reference(adjacency, tile_mask, out_grad, pre_two, hidden, pre_one, features, w_two, w_one):
    weight_scale = 4.0 * NODE_DEV ** -0.5
    grad_two = jnp.where(pre_two > 0, out_grad, jnp.zeros_like(out_grad))
    prop_two = propagate(adjacency, tile_mask, grad_two, N_ROW).astype(jnp.bfloat16)
    weight_grad_two = jnp.dot(hidden.T, prop_two, preferred_element_type=jnp.float32) * weight_scale
    back_grad = jnp.dot(prop_two, w_two.T, preferred_element_type=jnp.float32)
    grad_one = jnp.where(pre_one > 0, back_grad, jnp.zeros_like(back_grad)).astype(jnp.bfloat16)
    prop_one = propagate(adjacency, tile_mask, grad_one, N_COL).astype(jnp.bfloat16)
    weight_grad_one = jnp.dot(features.T, prop_one, preferred_element_type=jnp.float32) * weight_scale
    node_grad = jnp.dot(prop_one, w_one.T, preferred_element_type=jnp.float32).astype(jnp.bfloat16)
    return node_grad, weight_grad_one, weight_grad_two
```

```python
import functools

import jax
import jax.numpy as jnp
from jax import lax
from jax.experimental import pallas as pl
from jax.experimental.pallas import tpu as pltpu
from jax.sharding import PartitionSpec as P

MESH = pl.DeviceIdType.MESH
F32 = jnp.float32
BF16 = jnp.bfloat16
NT = (((1,), (1,)), ((), ()))
TN = (((0,), (0,)), ((), ()))


def mm(a, b):
    return jnp.dot(a, b, preferred_element_type=F32)


def kernel(
    n_row, n_col, tile, scale,
    adj_hbm, mask_hbm, og_hbm, p2_hbm, hid_hbm, p1_hbm, feat_hbm, w2_hbm, w1_hbm,
    node_out, wg1_out, wg2_out,
    graph, mask_v, mexp, small, gt, acc, sb, rb, gc, acc2, sd, rs, rd, e_src, e_r1, e_r2, e_sum, e_out,
    load_sem, gload_sem, a_s, a_r, b_s, b_r, c_s, c_r, ds_s, ds_r, d_s, d_r,
    e1_s, e1_r, e2_s, e2_r, e3_s, e3_r,
):
    row, col = lax.axis_index("row"), lax.axis_index("col")
    s = og_hbm.shape[0]
    h = s // 2
    y, zh = row // 2, lax.rem(row, 2)
    x, zl, core = col // 4, lax.rem(col // 2, 2), lax.rem(col, 2)

    def xor(a, k, bits):
        out = a * 0
        for i in range(bits):
            bit = lax.rem(a // (1 << i), 2)
            out = out + ((1 - bit) if (k >> i) & 1 else bit) * (1 << i)
        return out

    def col_at(dx, dz=0, dc=0):
        zz = (1 - zl) if dz else zl
        cc = (1 - core) if dc else core
        return lax.rem(x + dx + 4, 4) * 4 + zz * 2 + cc

    def row_at(dy, dz=0):
        zz = (1 - zh) if dz else zh
        return lax.rem(y + dy + 4, 4) * 2 + zz

    order = [
        (0, 0, 0), (0, 0, 1), (0, 1, 0), (-1, 0, 0), (1, 0, 0), (0, 1, 1), (-1, 0, 1), (1, 0, 1),
        (-1, 1, 0), (1, 1, 0), (-1, 1, 1), (1, 1, 1), (2, 0, 0), (2, 0, 1), (2, 1, 0), (2, 1, 1),
    ]

    names = [(og_hbm, 0), (p2_hbm, 1), (w2_hbm, 2), (p1_hbm, 3), (hid_hbm, 4), (feat_hbm, 5), (w1_hbm, 6)]
    loads = [pltpu.make_async_copy(ref, small.at[i], load_sem.at[i]) for ref, i in names]
    mload = pltpu.make_async_copy(mask_hbm, mask_v, load_sem.at[7])
    loads[0].start()
    loads[1].start()
    mload.start()
    gloads = []
    for i, o in enumerate(order):
        at = pl.ds(pl.multiple_of(col_at(*o) * s, s), s)
        cp = pltpu.make_async_copy(adj_hbm.at[at, :], graph.at[at, :], gload_sem.at[i])
        cp.start()
        gloads.append(cp)
    for cp in loads[2:]:
        cp.start()

    barrier = pltpu.get_barrier_semaphore()
    for k in range(1, n_col):
        pl.semaphore_signal(barrier, inc=1, device_id=(row, xor(col, k, 4)), device_id_type=MESH)
    for k in range(1, n_row):
        pl.semaphore_signal(barrier, inc=1, device_id=(xor(row, k, 3), col), device_id_type=MESH)

    loads[0].wait()
    loads[1].wait()
    own = jnp.where(small[1].astype(F32) > 0, small[0].astype(F32), 0.0)
    gt[col] = own.T.astype(BF16)
    mload.wait()
    width = mexp.shape[1]
    pick = (
        lax.broadcasted_iota(jnp.int32, (mask_v.shape[1], width), 1) // tile
        == lax.broadcasted_iota(jnp.int32, (mask_v.shape[1], width), 0)
    ).astype(F32)
    mexp[...] = mm(mask_v[...].astype(F32).astype(BF16), pick.astype(BF16))
    pl.semaphore_wait(barrier, n_col + n_row - 2)

    pending = []

    def send(src, dst, ss, rr, k, dev):
        cp = pltpu.make_async_remote_copy(
            src_ref=src, dst_ref=dst, send_sem=ss.at[k], recv_sem=rr.at[k],
            device_id=dev, device_id_type=MESH,
        )
        cp.start()
        pending.append(cp)
        return cp

    lo, hi = pl.ds(0, h), pl.ds(h, h)
    a_cp = {}

    def a_send(k, o, to, part=None):
        ref = gt.at[col_at(*o)] if part is None else gt.at[col_at(*o), part]
        a_cp[k] = send(ref, ref, a_s, a_r, k, (row, col_at(*to)))

    zp, xp, xm, sib = (0, 1, 0), (1, 0, 0), (-1, 0, 0), (0, 0, 1)
    a_send(0, (0, 0, 0), zp)
    a_send(1, (0, 0, 0), xp)
    a_send(2, (0, 0, 0), xm)
    a_send(3, (0, 0, 0), sib)

    def mask_chunk(i):
        o = order[i]
        gloads[i].wait()
        j = col_at(*o)
        for t in range(s // tile):
            m = mexp[pl.ds(j * (s // tile) + t, 1), :]
            m16 = jnp.broadcast_to(m, (16, width)).astype(BF16)

            @pl.loop(0, tile // 16)
            def _(g):
                at = pl.ds(pl.multiple_of(j * s + t * tile + g * 16, 16), 16)
                graph[at, :] = graph[at, :] * m16

    def mm1(idx, first=False):
        for i in idx:
            mask_chunk(i)
        js = [col_at(*order[i]) for i in idx]

        @pl.loop(0, n_row)
        def _(d):
            at = pl.ds(pl.multiple_of(d * s, s), s)
            total = None
            for j in js:
                p = mm(gt[j], graph[pl.ds(pl.multiple_of(j * s, s), s), at])
                total = p if total is None else total + p
            acc[d] = total if first else acc[d] + total

    mm1([0], True)
    a_cp[3].wait_recv()
    mm1([1])
    a_cp[0].wait_recv()
    a_send(4, (0, 1, 0), xp)
    a_send(5, (0, 1, 0), xm)
    a_send(6, (0, 1, 0), sib)
    a_cp[1].wait_recv()
    a_send(7, (-1, 0, 0), xp, lo)
    a_send(8, (-1, 0, 0), sib)
    a_cp[2].wait_recv()
    a_send(9, (1, 0, 0), xm, hi)
    a_send(10, (1, 0, 0), sib)
    mm1([2, 3])
    a_cp[6].wait_recv()
    mm1([4, 5])
    a_cp[4].wait_recv()
    a_send(11, (-1, 1, 0), xp, lo)
    a_send(12, (-1, 1, 0), sib)
    a_cp[5].wait_recv()
    a_send(13, (1, 1, 0), xm, hi)
    a_send(14, (1, 1, 0), sib)
    a_cp[8].wait_recv()
    a_cp[10].wait_recv()
    mm1([6, 7])
    mm1([8, 9])
    a_cp[7].wait_recv()
    a_cp[9].wait_recv()
    a_send(15, (2, 0, 0), sib)
    a_cp[12].wait_recv()
    a_cp[14].wait_recv()
    mm1([10, 11])
    a_cp[11].wait_recv()
    a_cp[13].wait_recv()
    a_send(16, (2, 1, 0), sib)
    a_cp[15].wait_recv()
    mm1([12, 13])
    a_cp[16].wait_recv()
    mm1([14, 15])

    def scatter(part, sbuf, rbuf, ss, rr, ring, slot):
        cp = {}

        def go(k, o, half, value, to):
            ref = sbuf.at[slot(*o), lo if half == 0 else hi]
            ref[...] = value.astype(BF16)
            cp[k] = send(ref, rbuf.at[k], ss, rr, k, ring(*to))

        for k, dz in ((0, 1), (2, 0)):
            go(k, (2, dz), 0, part(2, dz, 0), (1, 0))
            go(k + 1, (2, dz), 1, part(2, dz, 1), (-1, 0))
        for k, dz in ((4, 1), (6, 0)):
            go(k, (1, dz), 1, part(1, dz, 1), (1, 0))
            go(k + 1, (-1, dz), 0, part(-1, dz, 0), (-1, 0))
        for k, dz, b in ((8, 1, 0), (10, 0, 2)):
            cp[b].wait_recv()
            go(k, (1, dz), 0, part(1, dz, 0) + rbuf[b].astype(F32), (1, 0))
            cp[b + 1].wait_recv()
            go(k + 1, (-1, dz), 1, part(-1, dz, 1) + rbuf[b + 1].astype(F32), (-1, 0))
        for k in (4, 5, 8, 9):
            cp[k].wait_recv()
        go(12, (0, 1), 0, part(0, 1, 0) + rbuf[5].astype(F32) + rbuf[8].astype(F32), (0, 1))
        go(13, (0, 1), 1, part(0, 1, 1) + rbuf[4].astype(F32) + rbuf[9].astype(F32), (0, 1))
        for k in (6, 7, 10, 11):
            cp[k].wait_recv()
        top = part(0, 0, 0) + rbuf[7].astype(F32) + rbuf[10].astype(F32)
        low = part(0, 0, 1) + rbuf[6].astype(F32) + rbuf[11].astype(F32)
        cp[12].wait_recv()
        top = top + rbuf[12].astype(F32)
        cp[13].wait_recv()
        low = low + rbuf[13].astype(F32)
        return jnp.concatenate([top, low], axis=0)

    def part_b(dy, dz, half):
        return acc[row_at(dy, dz), lo if half == 0 else hi]

    prop_t = scatter(part_b, sb, rb, b_s, b_r, lambda dy, dz: (row_at(dy, dz), col), row_at)
    prop_two = prop_t.T.astype(BF16)

    for cp in loads[2:]:
        cp.wait()
    back = lax.dot_general(prop_two, small[2], NT, preferred_element_type=F32)
    gc[row] = jnp.where(small[3].astype(F32) > 0, back, 0.0).astype(BF16)
    c_cp = {}

    def c_send(k, o, to, part=None):
        ref = gc.at[row_at(*o)] if part is None else gc.at[row_at(*o), part]
        c_cp[k] = send(ref, ref, c_s, c_r, k, (row_at(*to), col))

    c_send(0, (0, 0), (0, 1))
    c_send(1, (0, 0), (1, 0))
    c_send(2, (0, 0), (-1, 0))

    e1, e2, e3 = {}, {}, {}

    def reduce_start(w, term):
        e_src[w] = term.reshape(e_src.shape[1:])
        for k in range(1, n_col):
            peer = xor(col, k, 4)
            e1[w, k] = send(e_src.at[w, peer], e_r1.at[w, k], e1_s.at[w], e1_r.at[w], k, (row, peer))

    def reduce_middle(w):
        total = e_src[w, col]
        for k in range(1, n_col):
            e1[w, k].wait_recv()
            total = total + e_r1[w, k]
        e_sum[w] = total
        for k in range(1, n_row):
            e2[w, k] = send(e_sum.at[w], e_r2.at[w, k], e2_s.at[w], e2_r.at[w], k, (xor(row, k, 3), col))

    def reduce_last(w):
        total = e_sum[w]
        for k in range(1, n_row):
            e2[w, k].wait_recv()
            total = total + e_r2[w, k]
        e_out[w, col] = total * scale
        for k in range(1, n_col):
            peer = xor(col, k, 4)
            e3[w, k] = send(e_out.at[w, col], e_out.at[w, col], e3_s.at[w], e3_r.at[w], k, (row, peer))

    def reduce_end(w, out):
        for k in range(1, n_col):
            e3[w, k].wait_recv()
        out[...] = e_out[w].reshape(out.shape)

    reduce_start(0, lax.dot_general(small[4], prop_two, TN, preferred_element_type=F32))

    def mm2(os, first=False):
        rs_ = [row_at(*o) for o in os]

        @pl.loop(0, n_col)
        def _(j):
            at = pl.ds(pl.multiple_of(j * s, s), s)
            total = None
            for r in rs_:
                p = mm(graph[at, pl.ds(pl.multiple_of(r * s, s), s)], gc[r])
                total = p if total is None else total + p
            acc2[j] = total if first else acc2[j] + total

    mm2([(0, 0)], True)
    c_cp[0].wait_recv()
    c_send(3, (0, 1), (1, 0))
    c_send(4, (0, 1), (-1, 0))
    c_cp[1].wait_recv()
    c_send(5, (-1, 0), (1, 0), lo)
    c_cp[2].wait_recv()
    c_send(6, (1, 0), (-1, 0), hi)
    mm2([(0, 1), (-1, 0)])
    c_cp[3].wait_recv()
    c_send(7, (-1, 1), (1, 0), lo)
    c_cp[4].wait_recv()
    c_send(8, (1, 1), (-1, 0), hi)
    mm2([(1, 0), (-1, 1)])
    reduce_middle(0)
    c_cp[5].wait_recv()
    c_cp[6].wait_recv()
    mm2([(1, 1), (2, 0)])
    c_cp[7].wait_recv()
    c_cp[8].wait_recv()

    last = row_at(2, 1)
    last_cols = pl.ds(pl.multiple_of(last * s, s), s)
    ring_order = [(2, 1), (2, 0), (1, 1), (-1, 1), (1, 0), (-1, 0), (0, 1), (0, 0)]
    ds_cp = {}
    for i, (dx, dz) in enumerate(ring_order):
        j = col_at(dx, dz, 1)
        total = acc2[j] + mm(graph[pl.ds(pl.multiple_of(j * s, s), s), last_cols], gc[last])
        sd[j] = total.astype(BF16)
        ds_cp[dx, dz] = send(sd.at[j], rs.at[i], ds_s, ds_r, i, (row, col_at(0, 0, 1)))
    for dx, dz in ring_order:
        j = col_at(dx, dz, 0)
        acc2[j] = acc2[j] + mm(graph[pl.ds(pl.multiple_of(j * s, s), s), last_cols], gc[last])

    arrived = set()

    def part_d(dx, dz, half):
        if (dx, dz) not in arrived:
            ds_cp[dx, dz].wait_recv()
            arrived.add((dx, dz))
        at = lo if half == 0 else hi
        return acc2[col_at(dx, dz), at] + rs[ring_order.index((dx, dz)), at].astype(F32)

    reduce_last(0)
    prop_one = scatter(part_d, sd, rd, d_s, d_r, lambda dx, dz: (row, col_at(dx, dz)), col_at).astype(BF16)
    reduce_start(1, lax.dot_general(small[5], prop_one, TN, preferred_element_type=F32))
    node_out[...] = lax.dot_general(prop_one, small[6], NT, preferred_element_type=F32).astype(BF16)
    reduce_end(0, wg2_out)
    reduce_middle(1)
    reduce_last(1)
    reduce_end(1, wg1_out)
    for cp in pending:
        cp.wait_send()


def local(adjacency, tile_mask, out_grad, pre_two, hidden, pre_one, features, w_two, w_one):
    n_row, n_col = lax.axis_size("row"), lax.axis_size("col")
    rows, cols = adjacency.shape
    s, f = out_grad.shape
    tile = rows // tile_mask.shape[0]
    scale = 4.0 * s ** (-0.5)
    h = s // 2
    sl = f // n_col
    dma = pltpu.SemaphoreType.DMA
    return pl.pallas_call(
        functools.partial(kernel, n_row, n_col, tile, scale),
        out_shape=(
            jax.ShapeDtypeStruct((s, f), BF16),
            jax.ShapeDtypeStruct((f, f), F32),
            jax.ShapeDtypeStruct((f, f), F32),
        ),
        in_specs=[pl.BlockSpec(memory_space=pl.ANY)] * 9,
        out_specs=[pl.BlockSpec(memory_space=pltpu.VMEM)] * 3,
        scratch_shapes=[
            pltpu.VMEM((rows, cols), BF16),
            pltpu.VMEM(tile_mask.shape, jnp.int32),
            pltpu.VMEM((tile_mask.shape[0], cols), F32),
            pltpu.VMEM((7, s, f), BF16),
            pltpu.VMEM((n_col, f, s), BF16),
            pltpu.VMEM((n_row, f, s), F32),
            pltpu.VMEM((n_row, f, s), BF16),
            pltpu.VMEM((14, h, f), BF16),
            pltpu.VMEM((n_row, s, f), BF16),
            pltpu.VMEM((n_col, s, f), F32),
            pltpu.VMEM((n_col, s, f), BF16),
            pltpu.VMEM((n_row, s, f), BF16),
            pltpu.VMEM((14, h, f), BF16),
            pltpu.VMEM((2, n_col, sl, f), F32),
            pltpu.VMEM((2, n_col, sl, f), F32),
            pltpu.VMEM((2, n_row, sl, f), F32),
            pltpu.VMEM((2, sl, f), F32),
            pltpu.VMEM((2, n_col, sl, f), F32),
            dma((8,)), dma((n_col,)), dma((17,)), dma((17,)), dma((14,)), dma((14,)), dma((9,)), dma((9,)),
            dma((8,)), dma((8,)), dma((14,)), dma((14,)),
            dma((2, n_col)), dma((2, n_col)), dma((2, n_row)), dma((2, n_row)), dma((2, n_col)), dma((2, n_col)),
        ],
        compiler_params=pltpu.CompilerParams(
            collective_id=0, has_side_effects=True, vmem_limit_bytes=56 << 20
        ),
    )(adjacency, tile_mask, out_grad, pre_two, hidden, pre_one, features, w_two, w_one)


def solution(mesh):
    return jax.shard_map(
        local,
        mesh=mesh,
        in_specs=(
            P("row", "col"),
            P("row", "col"),
            P(("row", "col"), None),
            P(("row", "col"), None),
            P(("col", "row"), None),
            P(("col", "row"), None),
            P(("row", "col"), None),
            P(),
            P(),
        ),
        out_specs=(P(("row", "col"), None), P(), P()),
        check_vma=False,
    )
```

```python
import functools

import jax
import jax.numpy as jnp
from jax import lax
from jax.experimental import pallas as pl
from jax.experimental.pallas import tpu as pltpu
from jax.sharding import PartitionSpec as P

MESH = pl.DeviceIdType.MESH
F32 = jnp.float32
BF16 = jnp.bfloat16
NT = (((1,), (1,)), ((), ()))
TN = (((0,), (0,)), ((), ()))


def mm(a, b):
    return jnp.dot(a, b, preferred_element_type=F32)


def kernel(
    n_row, n_col, tile, scale,
    adj_hbm, mask_hbm, og_hbm, p2_hbm, hid_hbm, p1_hbm, feat_hbm, w2_hbm, w1_hbm,
    node_out, wg1_out, wg2_out,
    graph, mask_v, mexp, small, gt, ft, acc, sb, rb, gc, acc2, sd, rs, rd,
    e_src, e_sib, e_half, e_r1, e_r2, e_sum, e_out,
    load_sem, gload_sem, s_s, s_r, f_s, f_r, a_s, a_r, b_s, b_r, c_s, c_r, ds_s, ds_r, d_s, d_r,
    e0_s, e0_r, e1_s, e1_r, e2_s, e2_r, e3_s, e3_r,
):
    row, col = lax.axis_index("row"), lax.axis_index("col")
    s = og_hbm.shape[0]
    h = s // 2
    y, zh = row // 2, lax.rem(row, 2)
    x, zl, core = col // 4, lax.rem(col // 2, 2), lax.rem(col, 2)

    def xor(a, k, bits):
        out = a * 0
        for i in range(bits):
            bit = lax.rem(a // (1 << i), 2)
            out = out + ((1 - bit) if (k >> i) & 1 else bit) * (1 << i)
        return out

    def col_at(dx, dz=0, dc=0):
        zz = (1 - zl) if dz else zl
        cc = (1 - core) if dc else core
        return lax.rem(x + dx + 4, 4) * 4 + zz * 2 + cc

    def row_at(dy, dz=0):
        zz = (1 - zh) if dz else zh
        return lax.rem(y + dy + 4, 4) * 2 + zz

    order = [
        (0, 0, 0), (0, 0, 1), (-1, 0, 0), (1, 0, 0), (-1, 0, 1), (1, 0, 1), (0, 1, 0), (0, 1, 1),
        (2, 0, 0), (2, 0, 1), (-1, 1, 0), (1, 1, 0), (-1, 1, 1), (1, 1, 1), (2, 1, 0), (2, 1, 1),
    ]

    names = [(og_hbm, 0), (p2_hbm, 1), (w2_hbm, 2), (p1_hbm, 3), (hid_hbm, 4), (feat_hbm, 5), (w1_hbm, 6)]
    loads = [pltpu.make_async_copy(ref, small.at[i], load_sem.at[i]) for ref, i in names]
    mload = pltpu.make_async_copy(mask_hbm, mask_v, load_sem.at[7])
    barrier = pltpu.get_barrier_semaphore()
    steps = ((1, 0), (-1, 0), (2, 0), (0, 1))
    hello = [(row, col_at(0, 0, 1))] + [(row, col_at(*o)) for o in steps] + [(row_at(*o), col) for o in steps]
    for dev in hello:
        pl.semaphore_signal(barrier, inc=1, device_id=dev, device_id_type=MESH)
    loads[0].start()
    loads[1].start()
    mload.start()
    gloads = []
    for i, o in enumerate(order):
        at = pl.ds(pl.multiple_of(col_at(*o) * s, s), s)
        cp = pltpu.make_async_copy(adj_hbm.at[at, :], graph.at[at, :], gload_sem.at[i])
        cp.start()
        gloads.append(cp)
    for cp in loads[2:]:
        cp.start()

    loads[0].wait()
    loads[1].wait()
    own = jnp.where(small[1].astype(F32) > 0, small[0].astype(F32), 0.0)
    gt[col] = own.T.astype(BF16)
    mload.wait()
    width = mexp.shape[1]
    pick = (
        lax.broadcasted_iota(jnp.int32, (mask_v.shape[0], width), 1) // tile
        == lax.broadcasted_iota(jnp.int32, (mask_v.shape[0], width), 0)
    ).astype(F32)
    mexp[...] = mm(mask_v[...].astype(F32).T.astype(BF16), pick.astype(BF16))
    pl.semaphore_wait(barrier, len(hello))

    pending = []

    def send(src, dst, ss, rr, k, dev):
        cp = pltpu.make_async_remote_copy(
            src_ref=src, dst_ref=dst, send_sem=ss.at[k], recv_sem=rr.at[k],
            device_id=dev, device_id_type=MESH,
        )
        cp.start()
        pending.append(cp)
        return cp

    lo, hi = pl.ds(0, h), pl.ds(h, h)
    halves = (lo, hi)

    def gather(buf, slot, dev, ss, rr):
        cp = {}

        def go(k, o, half, to):
            ref = buf.at[slot(*o), halves[half]]
            cp[k] = send(ref, ref, ss, rr, k, dev(*to))

        def start():
            go(0, (0, 0), 0, (0, 1))
            for k, d in ((1, 1), (2, -1), (3, 2)):
                go(k, (0, 0), 1, (d, 0))
            for k, d in ((4, 1), (5, -1), (6, 2)):
                go(k, (0, 0), 0, (d, 0))
            go(7, (0, 0), 1, (0, 1))

        def forward():
            cp[0].wait_recv()
            for k, d in ((8, 1), (9, -1), (10, 2)):
                go(k, (0, 1), 0, (d, 0))
            for k, d in ((1, -1), (2, 1), (3, 2)):
                cp[k].wait_recv()
                go(k + 10, (d, 0), 1, (0, 1))

        def near(d):
            cp[{-1: 4, 1: 5, 2: 6}[d]].wait_recv()

        def pair():
            cp[7].wait_recv()

        def far(d):
            k = {-1: 8, 1: 9, 2: 10}[d]
            cp[k].wait_recv()
            cp[k + 3].wait_recv()

        return start, forward, near, pair, far

    def scatter(part, sbuf, rbuf, slot, dev, ss, rr):
        cp = {}

        def go(k, o, half, value, to):
            ref = sbuf.at[slot(*o), halves[half]]
            ref[...] = value.astype(BF16)
            cp[k] = send(ref, rbuf.at[k], ss, rr, k, dev(*to))

        def got(k):
            cp[k].wait_recv()
            return rbuf[k].astype(F32)

        def one():
            for k, d in ((0, 1), (1, -1), (2, 2), (3, 0)):
                go(k, (d, 1), 1, part(d, 1, 1), (0, 1))
                if d:
                    go(k + 4, (d, 1), 0, part(d, 1, 0), (d, 0))
            for k, d in ((7, 1), (8, -1), (9, 2)):
                go(k, (d, 0), 0, part(d, 0, 0), (d, 0))

        def two():
            for k, d in ((0, 1), (1, -1), (2, 2)):
                go(k + 10, (d, 0), 1, part(d, 0, 1) + got(k), (d, 0))

        def three():
            go(13, (0, 1), 0, part(0, 1, 0) + got(4) + got(5) + got(6), (0, 1))

        def four():
            low = part(0, 0, 1) + got(3)
            top = part(0, 0, 0) + got(7) + got(8) + got(9)
            low = low + got(10) + got(11) + got(12)
            top = top + got(13)
            return jnp.concatenate([top, low], axis=0)

        return one, two, three, four

    def weight_reduce(w, inner, outer, me, both):
        cp = {}
        sib_dev = (row, col_at(0, 0, 1))

        def zero(term):
            e_src[w] = term.reshape(e_src.shape[1:])
            cp["a"] = send(e_src.at[w, 1 - core], e_sib.at[w], e0_s, e0_r, w, sib_dev)

        def one():
            cp["a"].wait_recv()
            e_half[w] = e_src[w, core] + e_sib[w]
            for k in range(1, n_row):
                cp[1, k] = send(e_half.at[w, xor(me, k, 3)], e_r1.at[w, k], e1_s.at[w], e1_r.at[w], k, inner(k))

        def two():
            total = e_half[w, me]
            for k in range(1, n_row):
                cp[1, k].wait_recv()
                total = total + e_r1[w, k]
            e_sum[w] = total
            for k in range(1, n_row):
                cp[2, k] = send(e_sum.at[w], e_r2.at[w, k], e2_s.at[w], e2_r.at[w], k, outer(k))

        def three():
            total = e_sum[w]
            for k in range(1, n_row):
                cp[2, k].wait_recv()
                total = total + e_r2[w, k]
            e_out[w, core, me] = total * scale
            ref = e_out.at[w, core, me]
            for k in range(1, n_row):
                cp[3, k] = send(ref, ref, e3_s.at[w, 0], e3_r.at[w, 0], k, inner(k))
            if both:
                cp["b"] = send(ref, ref, e0_s, e0_r, 2 + w, sib_dev)
                for k in range(1, n_row):
                    cp[4, k] = send(ref, ref, e3_s.at[w, 1], e3_r.at[w, 1], k, (inner(k)[0], col_at(0, 0, 1)))

        def four():
            for k in range(1, n_row):
                cp[3, k].wait_recv()
                if both:
                    cp[4, k].wait_recv()
            if both:
                return
            ref = e_out.at[w, core]
            cp["b"] = send(ref, ref, e0_s, e0_r, 2 + w, sib_dev)

        def five(out):
            cp["b"].wait_recv()
            out[...] = e_out[w].reshape(out.shape)

        return zero, one, two, three, four, five

    def row_dev(k):
        return (xor(row, k, 3), col)

    def col_dev(k):
        return (row, xor(col // 2, k, 3) * 2 + core)

    def in_row(dy, dz):
        return (row_at(dy, dz), col)

    def in_col(dx, dz):
        return (row, col_at(dx, dz))

    sib_dev = (row, col_at(0, 0, 1))
    s_cp = {}

    def to_sibling(buf, o, k):
        ref = buf.at[col_at(*o)]
        s_cp[k] = send(ref, ref, s_s, s_r, k, sib_dev)

    start, forward, near, pair, far = gather(gt, col_at, in_col, a_s, a_r)
    start()
    to_sibling(gt, (0, 0), 0)

    def mask_chunk(i):
        o = order[i]
        gloads[i].wait()
        j = col_at(*o)
        for t in range(s // tile):
            m = mexp[pl.ds(j * (s // tile) + t, 1), :]
            m16 = jnp.broadcast_to(m, (16, width)).astype(BF16)

            @pl.loop(0, tile // 16)
            def _(g):
                at = pl.ds(pl.multiple_of(j * s + t * tile + g * 16, 16), 16)
                graph[at, :] = graph[at, :] * m16

    def mm1(idx, first=False):
        js = [col_at(*order[i]) for i in idx]

        @pl.loop(0, n_row, unroll=8)
        def _(d):
            at = pl.ds(pl.multiple_of(d * s, s), s)
            total = None
            for j in js:
                p = mm(gt[j], graph[pl.ds(pl.multiple_of(j * s, s), s), at])
                total = p if total is None else total + p
            acc[d] = total if first else acc[d] + total

    mask_chunk(0)
    mask_chunk(1)
    s_cp[0].wait_recv()
    mm1([0, 1], True)
    forward()
    for i in (2, 3, 4, 5):
        mask_chunk(i)
    near(-1)
    to_sibling(gt, (-1, 0), 1)
    near(1)
    to_sibling(gt, (1, 0), 2)
    mm1([2, 3])
    pair()
    to_sibling(gt, (0, 1), 3)
    for i in (6, 7, 8, 9):
        mask_chunk(i)
    s_cp[1].wait_recv()
    s_cp[2].wait_recv()
    mm1([4, 5])
    near(2)
    to_sibling(gt, (2, 0), 4)
    s_cp[3].wait_recv()
    mm1([6, 7])
    for i in (10, 11, 12, 13, 14, 15):
        mask_chunk(i)
    far(-1)
    to_sibling(gt, (-1, 1), 5)
    far(1)
    to_sibling(gt, (1, 1), 6)
    s_cp[4].wait_recv()
    mm1([8, 9])
    far(2)
    to_sibling(gt, (2, 1), 7)
    s_cp[5].wait_recv()
    mm1([10, 11])
    s_cp[6].wait_recv()
    mm1([12, 13])
    s_cp[7].wait_recv()

    summed = set()

    def part_b(dy, dz, half):
        if (dy, dz) not in summed:
            summed.add((dy, dz))
            d = row_at(dy, dz)
            at = pl.ds(pl.multiple_of(d * s, s), s)
            j, jj = col_at(*order[14]), col_at(*order[15])
            acc[d] = (
                acc[d]
                + mm(gt[j], graph[pl.ds(pl.multiple_of(j * s, s), s), at])
                + mm(gt[jj], graph[pl.ds(pl.multiple_of(jj * s, s), s), at])
            )
        return acc[row_at(dy, dz), halves[half]]

    one, two, three, four = scatter(part_b, sb, rb, row_at, in_row, b_s, b_r)
    one()
    for cp in loads[2:]:
        cp.wait()
    ft[col] = small[5].astype(F32).T.astype(BF16)
    f_cp = {}

    def f_send(k, o, to):
        ref = ft.at[col_at(*o)]
        f_cp[k] = send(ref, ref, f_s, f_r, k, in_col(*to))

    f_send(0, (0, 0), (0, 1))
    f_send(1, (0, 0), (1, 0))
    f_send(2, (0, 0), (-1, 0))
    f_send(3, (0, 0), (2, 0))
    to_sibling(ft, (0, 0), 8)
    two()
    three()
    prop_two = four().T.astype(BF16)

    back = lax.dot_general(prop_two, small[2], NT, preferred_element_type=F32)
    gc[row] = jnp.where(small[3].astype(F32) > 0, back, 0.0).astype(BF16)
    start, forward, near, pair, far = gather(gc, row_at, in_row, c_s, c_r)
    start()
    w2_0, w2_1, w2_2, w2_3, w2_4, w2_5 = weight_reduce(0, col_dev, row_dev, col // 2, False)
    w2_0(lax.dot_general(small[4], prop_two, TN, preferred_element_type=F32))

    def mm2(os, first=False):
        rs_ = [row_at(*o) for o in os]

        @pl.loop(0, n_col, unroll=8)
        def _(j):
            at = pl.ds(pl.multiple_of(j * s, s), s)
            total = None
            for r in rs_:
                p = mm(graph[at, pl.ds(pl.multiple_of(r * s, s), s)], gc[r])
                total = p if total is None else total + p
            acc2[j] = total if first else acc2[j] + total

    f_cp[0].wait_recv()
    for k, d in ((4, 1), (5, -1), (6, 2)):
        f_send(k, (0, 1), (d, 0))
    to_sibling(ft, (0, 1), 9)
    w2_1()
    forward()
    mm2([(0, 0)], True)
    for k, d in ((1, -1), (2, 1), (3, 2)):
        f_cp[k].wait_recv()
        to_sibling(ft, (d, 0), 9 + k)
    near(-1)
    near(1)
    mm2([(-1, 0), (1, 0)])
    w2_2()
    near(2)
    pair()
    mm2([(2, 0), (0, 1)])
    for k, d in ((4, -1), (5, 1), (6, 2)):
        f_cp[k].wait_recv()
        to_sibling(ft, (d, 1), 9 + k)
    far(-1)
    far(1)
    mm2([(-1, 1), (1, 1)])
    w2_3()
    far(2)

    last = row_at(2, 1)
    last_cols = pl.ds(pl.multiple_of(last * s, s), s)
    ring_order = [(1, 1), (-1, 1), (2, 1), (0, 1), (1, 0), (-1, 0), (2, 0), (0, 0)]
    ds_cp = {}
    for i, (dx, dz) in enumerate(ring_order):
        j = col_at(dx, dz, 1)
        total = acc2[j] + mm(graph[pl.ds(pl.multiple_of(j * s, s), s), last_cols], gc[last])
        sd[j] = total.astype(BF16)
        ds_cp[dx, dz] = send(sd.at[j], rs.at[i], ds_s, ds_r, i, sib_dev)
    for dx, dz in ring_order:
        j = col_at(dx, dz, 0)
        acc2[j] = acc2[j] + mm(graph[pl.ds(pl.multiple_of(j * s, s), s), last_cols], gc[last])

    arrived = set()

    def part_d(dx, dz, half):
        if (dx, dz) not in arrived:
            ds_cp[dx, dz].wait_recv()
            arrived.add((dx, dz))
        at = halves[half]
        return acc2[col_at(dx, dz), at] + rs[ring_order.index((dx, dz)), at].astype(F32)

    one, two, three, four = scatter(part_d, sd, rd, col_at, in_col, d_s, d_r)
    one()
    for k in range(8, 16):
        s_cp[k].wait_recv()
    term = None
    for dx, dz in ring_order:
        j, jj = col_at(dx, dz, 0), col_at(dx, dz, 1)
        p = mm(ft[j], acc2[j].astype(BF16)) + mm(ft[jj], sd[jj])
        term = p if term is None else term + p
    w1_0, w1_1, w1_2, w1_3, w1_4, w1_5 = weight_reduce(1, row_dev, col_dev, row, True)
    w1_0(term)
    w2_4()
    w1_1()
    two()
    w1_2()
    three()
    w1_3()
    prop_one = four().astype(BF16)
    node_out[...] = lax.dot_general(prop_one, small[6], NT, preferred_element_type=F32).astype(BF16)
    w2_5(wg2_out)
    w1_4()
    w1_5(wg1_out)
    for cp in pending:
        cp.wait_send()


def finish(node_in, wg1_in, wg2_in, node_out, wg1_out, wg2_out, node, wg, sem):
    refs = ((node_in, node, node_out), (wg1_in, wg.at[0], wg1_out), (wg2_in, wg.at[1], wg2_out))
    ins = [pltpu.make_async_copy(a, b, sem.at[0, i]) for i, (a, b, _) in enumerate(refs)]
    outs = [pltpu.make_async_copy(b, c, sem.at[1, i]) for i, (_, b, c) in enumerate(refs)]
    for cp in ins:
        cp.start()
    for cp, out in zip(ins, outs):
        cp.wait()
        out.start()
    for out in outs:
        out.wait()


def local(adjacency, tile_mask, out_grad, pre_two, hidden, pre_one, features, w_two, w_one):
    n_row, n_col = lax.axis_size("row"), lax.axis_size("col")
    rows, cols = adjacency.shape
    s, f = out_grad.shape
    tile = rows // tile_mask.shape[0]
    scale = 4.0 * s ** (-0.5)
    h = s // 2
    sl = f // n_col
    dma = pltpu.SemaphoreType.DMA
    outs = pl.pallas_call(
        functools.partial(kernel, n_row, n_col, tile, scale),
        out_shape=(
            jax.ShapeDtypeStruct((s, f), BF16),
            jax.ShapeDtypeStruct((f, f), F32),
            jax.ShapeDtypeStruct((f, f), F32),
        ),
        in_specs=[pl.BlockSpec(memory_space=pl.ANY)] * 9,
        out_specs=[pl.BlockSpec(memory_space=pltpu.VMEM)] * 3,
        scratch_shapes=[
            pltpu.VMEM((rows, cols), BF16),
            pltpu.VMEM(tile_mask.shape[::-1], jnp.int32),
            pltpu.VMEM((tile_mask.shape[0], cols), F32),
            pltpu.VMEM((7, s, f), BF16),
            pltpu.VMEM((n_col, f, s), BF16),
            pltpu.VMEM((n_col, f, s), BF16),
            pltpu.VMEM((n_row, f, s), F32),
            pltpu.VMEM((n_row, f, s), BF16),
            pltpu.VMEM((14, h, f), BF16),
            pltpu.VMEM((n_row, s, f), BF16),
            pltpu.VMEM((n_col, s, f), F32),
            pltpu.VMEM((n_col, s, f), BF16),
            pltpu.VMEM((n_row, s, f), BF16),
            pltpu.VMEM((14, h, f), BF16),
            pltpu.VMEM((2, 2, n_row, sl, f), F32),
            pltpu.VMEM((2, n_row, sl, f), F32),
            pltpu.VMEM((2, n_row, sl, f), F32),
            pltpu.VMEM((2, n_row, sl, f), F32),
            pltpu.VMEM((2, n_row, sl, f), F32),
            pltpu.VMEM((2, sl, f), F32),
            pltpu.VMEM((2, 2, n_row, sl, f), F32),
            dma((8,)), dma((n_col,)), dma((16,)), dma((16,)), dma((7,)), dma((7,)),
            dma((14,)), dma((14,)), dma((14,)), dma((14,)), dma((14,)), dma((14,)),
            dma((8,)), dma((8,)), dma((14,)), dma((14,)),
            dma((4,)), dma((4,)), dma((2, n_row)), dma((2, n_row)), dma((2, n_row)), dma((2, n_row)),
            dma((2, 2, n_row)), dma((2, 2, n_row)),
        ],
        compiler_params=pltpu.CompilerParams(
            collective_id=0, has_side_effects=True, vmem_limit_bytes=56 << 20
        ),
    )(adjacency, tile_mask.T, out_grad, pre_two, hidden, pre_one, features, w_two, w_one)
    return pl.pallas_call(
        finish,
        out_shape=tuple(jax.ShapeDtypeStruct(o.shape, o.dtype) for o in outs),
        in_specs=[pl.BlockSpec(memory_space=pl.ANY)] * 3,
        out_specs=[pl.BlockSpec(memory_space=pl.ANY)] * 3,
        scratch_shapes=[
            pltpu.VMEM(outs[0].shape, BF16), pltpu.VMEM((2,) + outs[1].shape, F32), dma((2, 3)),
        ],
        compiler_params=pltpu.CompilerParams(vmem_limit_bytes=56 << 20),
    )(*outs)


def solution(mesh):
    return jax.shard_map(
        local,
        mesh=mesh,
        in_specs=(
            P("row", "col"),
            P("row", "col"),
            P(("row", "col"), None),
            P(("row", "col"), None),
            P(("col", "row"), None),
            P(("col", "row"), None),
            P(("row", "col"), None),
            P(),
            P(),
        ),
        out_specs=(P(("row", "col"), None), P(), P()),
        check_vma=False,
    )
```

```python
import functools

import jax
import jax.numpy as jnp
from jax import lax
from jax.experimental import pallas as pl
from jax.experimental.pallas import tpu as pltpu
from jax.sharding import PartitionSpec as P

MESH = pl.DeviceIdType.MESH
F32 = jnp.float32
BF16 = jnp.bfloat16
NT = (((1,), (1,)), ((), ()))
TN = (((0,), (0,)), ((), ()))


def mm(a, b):
    return jnp.dot(a, b, preferred_element_type=F32)


def kernel(
    n_row, n_col, tile, scale,
    adj_hbm, mask_hbm, og_hbm, p2_hbm, hid_hbm, p1_hbm, feat_hbm, w2_hbm, w1_hbm,
    node_out, wg1_out, wg2_out,
    graph, mask_v, mexp, small, gt, ft, acc, sb, rb, gc, acc2, sd, rs, rd,
    e_src, e_sib, e_half, e_r, e_all, e_out,
    load_sem, gload_sem, s_s, s_r, f_s, f_r, a_s, a_r, b_s, b_r, c_s, c_r, ds_s, ds_r, d_s, d_r,
    e0_s, e0_r, e1_s, e1_r,
):
    row, col = lax.axis_index("row"), lax.axis_index("col")
    s = og_hbm.shape[0]
    h = s // 2
    y, zh = row // 2, lax.rem(row, 2)
    x, zl, core = col // 4, lax.rem(col // 2, 2), lax.rem(col, 2)

    def col_at(dx, dz=0, dc=0):
        zz = (1 - zl) if dz else zl
        cc = (1 - core) if dc else core
        return lax.rem(x + dx + 4, 4) * 4 + zz * 2 + cc

    def row_at(dy, dz=0):
        zz = (1 - zh) if dz else zh
        return lax.rem(y + dy + 4, 4) * 2 + zz

    order = [
        (0, 0, 0), (0, 0, 1), (-1, 0, 0), (1, 0, 0), (-1, 0, 1), (1, 0, 1), (0, 1, 0), (0, 1, 1),
        (2, 0, 0), (2, 0, 1), (-1, 1, 0), (1, 1, 0), (-1, 1, 1), (1, 1, 1), (2, 1, 0), (2, 1, 1),
    ]

    names = [(og_hbm, 0), (p2_hbm, 1), (w2_hbm, 2), (p1_hbm, 3), (hid_hbm, 4), (feat_hbm, 5), (w1_hbm, 6)]
    loads = [pltpu.make_async_copy(ref, small.at[i], load_sem.at[i]) for ref, i in names]
    mload = pltpu.make_async_copy(mask_hbm, mask_v, load_sem.at[7])
    barrier = pltpu.get_barrier_semaphore()
    steps = ((1, 0), (-1, 0), (2, 0), (0, 1))
    hello = [(row, col_at(0, 0, 1))] + [(row, col_at(*o)) for o in steps] + [(row_at(*o), col) for o in steps]
    for dev in hello:
        pl.semaphore_signal(barrier, inc=1, device_id=dev, device_id_type=MESH)
    loads[0].start()
    loads[1].start()
    mload.start()
    gloads = []
    for i, o in enumerate(order):
        at = pl.ds(pl.multiple_of(col_at(*o) * s, s), s)
        cp = pltpu.make_async_copy(adj_hbm.at[at, :], graph.at[at, :], gload_sem.at[i])
        cp.start()
        gloads.append(cp)
    for cp in loads[2:]:
        cp.start()

    loads[0].wait()
    loads[1].wait()
    own = jnp.where(small[1].astype(F32) > 0, small[0].astype(F32), 0.0)
    gt[col] = own.T.astype(BF16)
    mload.wait()
    width = mexp.shape[1]
    pick = (
        lax.broadcasted_iota(jnp.int32, (mask_v.shape[0], width), 1) // tile
        == lax.broadcasted_iota(jnp.int32, (mask_v.shape[0], width), 0)
    ).astype(F32)
    mexp[...] = mm(mask_v[...].astype(F32).T.astype(BF16), pick.astype(BF16))
    pl.semaphore_wait(barrier, len(hello))

    pending = []

    def send(src, dst, ss, rr, k, dev):
        cp = pltpu.make_async_remote_copy(
            src_ref=src, dst_ref=dst, send_sem=ss.at[k], recv_sem=rr.at[k],
            device_id=dev, device_id_type=MESH,
        )
        cp.start()
        pending.append(cp)
        return cp

    lo, hi = pl.ds(0, h), pl.ds(h, h)
    halves = (lo, hi)

    def gather(buf, slot, dev, ss, rr):
        cp = {}

        def go(k, o, half, to):
            ref = buf.at[slot(*o), halves[half]]
            cp[k] = send(ref, ref, ss, rr, k, dev(*to))

        def start():
            go(0, (0, 0), 0, (0, 1))
            for k, d in ((1, 1), (2, -1), (3, 2)):
                go(k, (0, 0), 1, (d, 0))
            for k, d in ((4, 1), (5, -1), (6, 2)):
                go(k, (0, 0), 0, (d, 0))
            go(7, (0, 0), 1, (0, 1))

        def forward():
            cp[0].wait_recv()
            for k, d in ((8, 1), (9, -1), (10, 2)):
                go(k, (0, 1), 0, (d, 0))
            for k, d in ((1, -1), (2, 1), (3, 2)):
                cp[k].wait_recv()
                go(k + 10, (d, 0), 1, (0, 1))

        def near(d):
            cp[{-1: 4, 1: 5, 2: 6}[d]].wait_recv()

        def pair():
            cp[7].wait_recv()

        def far(d):
            k = {-1: 8, 1: 9, 2: 10}[d]
            cp[k].wait_recv()
            cp[k + 3].wait_recv()

        return start, forward, near, pair, far

    def scatter(part, sbuf, rbuf, slot, dev, ss, rr):
        cp = {}

        def go(k, o, half, value, to):
            ref = sbuf.at[slot(*o), halves[half]]
            ref[...] = value.astype(BF16)
            cp[k] = send(ref, rbuf.at[k], ss, rr, k, dev(*to))

        def got(k):
            cp[k].wait_recv()
            return rbuf[k].astype(F32)

        def one():
            for k, d in ((0, 1), (1, -1), (2, 2), (3, 0)):
                go(k, (d, 1), 1, part(d, 1, 1), (0, 1))
                if d:
                    go(k + 4, (d, 1), 0, part(d, 1, 0), (d, 0))
            for k, d in ((7, 1), (8, -1), (9, 2)):
                go(k, (d, 0), 0, part(d, 0, 0), (d, 0))

        def two():
            for k, d in ((0, 1), (1, -1), (2, 2)):
                go(k + 10, (d, 0), 1, part(d, 0, 1) + got(k), (d, 0))

        def three():
            go(13, (0, 1), 0, part(0, 1, 0) + got(4) + got(5) + got(6), (0, 1))

        def four():
            low = part(0, 0, 1) + got(3)
            top = part(0, 0, 0) + got(7) + got(8) + got(9)
            low = low + got(10) + got(11) + got(12)
            top = top + got(13)
            return jnp.concatenate([top, low], axis=0)

        return one, two, three, four

    ring = ((0, 1), (1, -1), (2, 2))
    flips = ((0, 0, 1), (1, 1, 0), (2, 1, 1))

    def weight_reduce(w, p, q, inner, outer, both):
        cp = {}
        sib_dev = (row, col_at(0, 0, 1))

        def zero_send(term):
            e_src[w, 1 - core] = term.reshape(e_src.shape[2:])
            cp["a"] = send(e_src.at[w, 1 - core], e_sib.at[w], e0_s, e0_r, w, sib_dev)

        def zero_keep(term):
            e_src[w, core] = term.reshape(e_src.shape[2:])

        def one():
            cp["a"].wait_recv()
            total = e_src[w, core] + e_sib[w]
            e_src[w, core] = total
            e_half[w] = total.astype(BF16)
            for k, d in ring:
                src = e_half.at[w, lax.rem(p + d + 4, 4)]
                cp[1, k] = send(src, e_r.at[w, k], e1_s.at[w, 0], e1_r.at[w, 0], k, inner(d))

        def share(stage, at, total, peers):
            ref = e_all.at[w, stage, at]
            ref[...] = total.astype(BF16)
            for k, dev in peers:
                cp[stage + 2, k] = send(ref, ref, e1_s.at[w, stage + 1], e1_r.at[w, stage + 1], k, dev)

        def gathered(stage):
            for k in range(3):
                cp[stage + 2, k].wait_recv()
            v = [e_all[w, stage, k].astype(F32) for k in range(4)]
            return (v[0] + v[1]) + (v[2] + v[3])

        def two():
            total = e_src[w, core, p]
            for k in range(3):
                cp[1, k].wait_recv()
                total = total + e_r[w, k].astype(F32)
            share(0, zh * 2 + zl, total, [(k, (row_at(0, dh), col_at(0, dl))) for k, dh, dl in flips])

        def three():
            share(1, q, gathered(0), [(k, outer(d)) for k, d in ring])

        def four():
            e_out[w, core, p] = (gathered(1) * scale).astype(BF16)
            ref = e_out.at[w, core, p]
            for k, d in ring:
                cp[4, k] = send(ref, ref, e1_s.at[w, 3], e1_r.at[w, 3], k, inner(d))
            if both:
                cp["b"] = send(ref, ref, e0_s, e0_r, 2 + w, sib_dev)
                for k, d in ring:
                    dev = (inner(d)[0], col_at(0, 0, 1))
                    cp[5, k] = send(ref, ref, e1_s.at[w, 4], e1_r.at[w, 4], k, dev)

        def five():
            for k in range(3):
                cp[4, k].wait_recv()
                if both:
                    cp[5, k].wait_recv()
            if both:
                return
            ref = e_out.at[w, core]
            cp["b"] = send(ref, ref, e0_s, e0_r, 2 + w, sib_dev)

        def six(out):
            cp["b"].wait_recv()
            out[...] = e_out[w].reshape(out.shape).astype(F32)

        return zero_send, zero_keep, one, two, three, four, five, six

    def in_row(dy, dz):
        return (row_at(dy, dz), col)

    def in_col(dx, dz):
        return (row, col_at(dx, dz))

    sib_dev = (row, col_at(0, 0, 1))
    s_cp = {}

    def to_sibling(buf, o, k):
        ref = buf.at[col_at(*o)]
        s_cp[k] = send(ref, ref, s_s, s_r, k, sib_dev)

    start, forward, near, pair, far = gather(gt, col_at, in_col, a_s, a_r)
    start()
    to_sibling(gt, (0, 0), 0)

    def mask_chunk(i):
        o = order[i]
        gloads[i].wait()
        j = col_at(*o)
        for t in range(s // tile):
            m = mexp[pl.ds(j * (s // tile) + t, 1), :]
            m16 = jnp.broadcast_to(m, (16, width)).astype(BF16)

            @pl.loop(0, tile // 16)
            def _(g):
                at = pl.ds(pl.multiple_of(j * s + t * tile + g * 16, 16), 16)
                graph[at, :] = graph[at, :] * m16

    def mm1(idx, first=False):
        js = [col_at(*order[i]) for i in idx]

        @pl.loop(0, n_row, unroll=8)
        def _(d):
            at = pl.ds(pl.multiple_of(d * s, s), s)
            total = None
            for j in js:
                p = mm(gt[j], graph[pl.ds(pl.multiple_of(j * s, s), s), at])
                total = p if total is None else total + p
            acc[d] = total if first else acc[d] + total

    mask_chunk(0)
    mask_chunk(1)
    s_cp[0].wait_recv()
    mm1([0, 1], True)
    forward()
    for i in (2, 3, 4, 5):
        mask_chunk(i)
    near(-1)
    to_sibling(gt, (-1, 0), 1)
    near(1)
    to_sibling(gt, (1, 0), 2)
    mm1([2, 3])
    pair()
    to_sibling(gt, (0, 1), 3)
    for i in (6, 7, 8, 9):
        mask_chunk(i)
    s_cp[1].wait_recv()
    s_cp[2].wait_recv()
    mm1([4, 5])
    near(2)
    to_sibling(gt, (2, 0), 4)
    s_cp[3].wait_recv()
    mm1([6, 7])
    for i in (10, 11, 12, 13, 14, 15):
        mask_chunk(i)
    far(-1)
    to_sibling(gt, (-1, 1), 5)
    far(1)
    to_sibling(gt, (1, 1), 6)
    s_cp[4].wait_recv()
    mm1([8, 9])
    far(2)
    to_sibling(gt, (2, 1), 7)
    s_cp[5].wait_recv()
    mm1([10, 11])
    s_cp[6].wait_recv()
    mm1([12, 13])
    s_cp[7].wait_recv()

    summed = set()

    def part_b(dy, dz, half):
        if (dy, dz) not in summed:
            summed.add((dy, dz))
            d = row_at(dy, dz)
            at = pl.ds(pl.multiple_of(d * s, s), s)
            j, jj = col_at(*order[14]), col_at(*order[15])
            acc[d] = (
                acc[d]
                + mm(gt[j], graph[pl.ds(pl.multiple_of(j * s, s), s), at])
                + mm(gt[jj], graph[pl.ds(pl.multiple_of(jj * s, s), s), at])
            )
        return acc[row_at(dy, dz), halves[half]]

    one, two, three, four = scatter(part_b, sb, rb, row_at, in_row, b_s, b_r)
    one()
    for cp in loads[2:]:
        cp.wait()
    ft[col] = small[5].astype(F32).T.astype(BF16)
    f_cp = {}

    def f_send(k, o, to):
        ref = ft.at[col_at(*o)]
        f_cp[k] = send(ref, ref, f_s, f_r, k, in_col(*to))

    two()
    f_send(0, (0, 0), (0, 1))
    f_send(1, (0, 0), (1, 0))
    f_send(2, (0, 0), (-1, 0))
    f_send(3, (0, 0), (2, 0))
    to_sibling(ft, (0, 0), 8)
    three()
    prop_two = four().T.astype(BF16)

    back = lax.dot_general(prop_two, small[2], NT, preferred_element_type=F32)
    gc[row] = jnp.where(small[3].astype(F32) > 0, back, 0.0).astype(BF16)
    start, forward, near, pair, far = gather(gc, row_at, in_row, c_s, c_r)
    start()
    w2_s, w2_k, w2_1, w2_2, w2_3, w2_4, w2_5, w2_6 = weight_reduce(
        0, x, y, lambda d: in_col(d, 0), lambda d: in_row(d, 0), False
    )
    e_src[0] = lax.dot_general(small[4], prop_two, TN, preferred_element_type=F32).reshape(e_src.shape[1:])
    w2_s(e_src[0, 1 - core])

    def mm2(os, first=False):
        rs_ = [row_at(*o) for o in os]

        @pl.loop(0, n_col, unroll=8)
        def _(j):
            at = pl.ds(pl.multiple_of(j * s, s), s)
            total = None
            for r in rs_:
                p = mm(graph[at, pl.ds(pl.multiple_of(r * s, s), s)], gc[r])
                total = p if total is None else total + p
            acc2[j] = total if first else acc2[j] + total

    f_cp[0].wait_recv()
    for k, d in ((4, 1), (5, -1), (6, 2)):
        f_send(k, (0, 1), (d, 0))
    to_sibling(ft, (0, 1), 9)
    w2_1()
    forward()
    mm2([(0, 0)], True)
    for k, d in ((1, -1), (2, 1), (3, 2)):
        f_cp[k].wait_recv()
        to_sibling(ft, (d, 0), 9 + k)
    near(-1)
    near(1)
    mm2([(-1, 0), (1, 0)])
    w2_2()
    near(2)
    pair()
    mm2([(2, 0), (0, 1)])
    w2_3()
    for k, d in ((4, -1), (5, 1), (6, 2)):
        f_cp[k].wait_recv()
        to_sibling(ft, (d, 1), 9 + k)
    far(-1)
    far(1)
    mm2([(-1, 1), (1, 1)])
    far(2)

    last = row_at(2, 1)
    last_cols = pl.ds(pl.multiple_of(last * s, s), s)
    ring_order = [(1, 1), (-1, 1), (2, 1), (0, 1), (1, 0), (-1, 0), (2, 0), (0, 0)]
    ds_cp = {}
    for i, (dx, dz) in enumerate(ring_order):
        j = col_at(dx, dz, 1)
        total = acc2[j] + mm(graph[pl.ds(pl.multiple_of(j * s, s), s), last_cols], gc[last])
        sd[j] = total.astype(BF16)
        ds_cp[dx, dz] = send(sd.at[j], rs.at[i], ds_s, ds_r, i, sib_dev)
    for dx, dz in ring_order:
        j = col_at(dx, dz, 0)
        acc2[j] = acc2[j] + mm(graph[pl.ds(pl.multiple_of(j * s, s), s), last_cols], gc[last])

    arrived = set()

    def part_d(dx, dz, half):
        if (dx, dz) not in arrived:
            ds_cp[dx, dz].wait_recv()
            arrived.add((dx, dz))
        at = halves[half]
        return acc2[col_at(dx, dz), at] + rs[ring_order.index((dx, dz)), at].astype(F32)

    one, two, three, four = scatter(part_d, sd, rd, col_at, in_col, d_s, d_r)
    one()
    for k in range(8, 16):
        s_cp[k].wait_recv()
    half_rows = ft.shape[1] // 2

    def term(which):
        at = pl.ds(pl.multiple_of(which * half_rows, half_rows), half_rows)
        total = None
        for dx, dz in ring_order:
            j, jj = col_at(dx, dz, 0), col_at(dx, dz, 1)
            p = mm(ft[j, at], acc2[j].astype(BF16)) + mm(ft[jj, at], sd[jj])
            total = p if total is None else total + p
        return total

    w1_s, w1_k, w1_1, w1_2, w1_3, w1_4, w1_5, w1_6 = weight_reduce(
        1, y, x, lambda d: in_row(d, 0), lambda d: in_col(d, 0), True
    )
    w1_s(term(1 - core))
    w1_k(term(core))
    w1_1()
    two()
    w1_2()
    three()
    w1_3()
    w2_4()
    prop_one = four().astype(BF16)
    w1_4()
    w2_5()
    node_out[...] = lax.dot_general(prop_one, small[6], NT, preferred_element_type=F32).astype(BF16)
    w2_6(wg2_out)
    w1_5()
    w1_6(wg1_out)
    for cp in pending:
        cp.wait_send()


def finish(node_in, wg1_in, wg2_in, node_out, wg1_out, wg2_out, node, wg, sem):
    refs = ((node_in, node, node_out), (wg1_in, wg.at[0], wg1_out), (wg2_in, wg.at[1], wg2_out))
    ins = [pltpu.make_async_copy(a, b, sem.at[0, i]) for i, (a, b, _) in enumerate(refs)]
    outs = [pltpu.make_async_copy(b, c, sem.at[1, i]) for i, (_, b, c) in enumerate(refs)]
    for cp in ins:
        cp.start()
    for cp, out in zip(ins, outs):
        cp.wait()
        out.start()
    for out in outs:
        out.wait()


def local(adjacency, tile_mask, out_grad, pre_two, hidden, pre_one, features, w_two, w_one):
    n_row, n_col = lax.axis_size("row"), lax.axis_size("col")
    rows, cols = adjacency.shape
    s, f = out_grad.shape
    tile = rows // tile_mask.shape[0]
    scale = 4.0 * s ** (-0.5)
    h = s // 2
    sl = f // 8
    dma = pltpu.SemaphoreType.DMA
    outs = pl.pallas_call(
        functools.partial(kernel, n_row, n_col, tile, scale),
        out_shape=(
            jax.ShapeDtypeStruct((s, f), BF16),
            jax.ShapeDtypeStruct((f, f), F32),
            jax.ShapeDtypeStruct((f, f), F32),
        ),
        in_specs=[pl.BlockSpec(memory_space=pl.ANY)] * 9,
        out_specs=[pl.BlockSpec(memory_space=pltpu.VMEM)] * 3,
        scratch_shapes=[
            pltpu.VMEM((rows, cols), BF16),
            pltpu.VMEM(tile_mask.shape[::-1], jnp.int32),
            pltpu.VMEM((tile_mask.shape[0], cols), F32),
            pltpu.VMEM((7, s, f), BF16),
            pltpu.VMEM((n_col, f, s), BF16),
            pltpu.VMEM((n_col, f, s), BF16),
            pltpu.VMEM((n_row, f, s), F32),
            pltpu.VMEM((n_row, f, s), BF16),
            pltpu.VMEM((14, h, f), BF16),
            pltpu.VMEM((n_row, s, f), BF16),
            pltpu.VMEM((n_col, s, f), F32),
            pltpu.VMEM((n_col, s, f), BF16),
            pltpu.VMEM((n_row, s, f), BF16),
            pltpu.VMEM((14, h, f), BF16),
            pltpu.VMEM((2, 2, 4, sl, f), F32),
            pltpu.VMEM((2, 4, sl, f), F32),
            pltpu.VMEM((2, 4, sl, f), BF16),
            pltpu.VMEM((2, 3, sl, f), BF16),
            pltpu.VMEM((2, 2, 4, sl, f), BF16),
            pltpu.VMEM((2, 2, 4, sl, f), BF16),
            dma((8,)), dma((n_col,)), dma((16,)), dma((16,)), dma((7,)), dma((7,)),
            dma((14,)), dma((14,)), dma((14,)), dma((14,)), dma((14,)), dma((14,)),
            dma((8,)), dma((8,)), dma((14,)), dma((14,)),
            dma((4,)), dma((4,)), dma((2, 5, 3)), dma((2, 5, 3)),
        ],
        compiler_params=pltpu.CompilerParams(
            collective_id=0, has_side_effects=True, vmem_limit_bytes=56 << 20
        ),
    )(adjacency, tile_mask.T, out_grad, pre_two, hidden, pre_one, features, w_two, w_one)
    return pl.pallas_call(
        finish,
        out_shape=tuple(jax.ShapeDtypeStruct(o.shape, o.dtype) for o in outs),
        in_specs=[pl.BlockSpec(memory_space=pl.ANY)] * 3,
        out_specs=[pl.BlockSpec(memory_space=pl.ANY)] * 3,
        scratch_shapes=[
            pltpu.VMEM(outs[0].shape, BF16), pltpu.VMEM((2,) + outs[1].shape, F32), dma((2, 3)),
        ],
        compiler_params=pltpu.CompilerParams(vmem_limit_bytes=56 << 20),
    )(*outs)


def solution(mesh):
    return jax.shard_map(
        local,
        mesh=mesh,
        in_specs=(
            P("row", "col"),
            P("row", "col"),
            P(("row", "col"), None),
            P(("row", "col"), None),
            P(("col", "row"), None),
            P(("col", "row"), None),
            P(("row", "col"), None),
            P(),
            P(),
        ),
        out_specs=(P(("row", "col"), None), P(), P()),
        check_vma=False,
    )
```
